32 devices in a mesh: prow: 2 (over y), pcol: 16 (over z, x, core).
Axes of the slice: x: 2, y: 2, z: 4, core: 2. Of those that a mesh axis runs over, the one named last changes fastest.
Arguments:
- ancestor_inverse: bfloat16 [24576, 24576], P('prow', 'pcol'), may hold values from -6 to 6
- tile_pattern: int32 [64, 64], replicated, may hold values 0 or 1
- rows_first: int32 [24576], replicated, may hold values 0 or 1
- rows_second: int32 [24576], replicated, may hold values 0 or 1
- panel_first: bfloat16 [24576, 512], P('prow', 'pcol'), may hold values from -0.0390625 to 0.0390625
- panel_second: bfloat16 [24576, 512], P('prow', 'pcol'), may hold values from -0.15625 to 0.15625
- inner_panel: bfloat16 [512, 512], replicated, may hold values from -0.25 to 0.25
- pivot_first: float32 [512, 512], replicated, may hold values from -6 to 6
- pivot_second: float32 [512, 512], replicated, may hold values from -6 to 6
Outputs:
- column_first: bfloat16 [24576, 512], P(('prow', 'pcol'))
- diagonal_first: float32 [512, 512], replicated
- inner_second: float32 [512, 512], replicated
- column_second: bfloat16 [24576, 512], P(('prow', 'pcol'))
- diagonal_second: float32 [512, 512], replicated
The draws below stay inside these ranges and needn't reach their ends.
Inputs may be any that keep to these rules, and one draw needn't show every extreme that they name: `tile_pattern`: 1 marks a structurally nonzero tile. `rows_first`: 1 marks a row of the first supernode's structure. By construction here, a row belongs to the second supernode's structure only where both rows_second and rows_first are 1.
All inputs are finite; a program needn't handle non-finite values.
Results may differ from the reference program's by a relative error of at most 0.015.
Values may be sent and summed in bfloat16 or wider, within the bound.
No kernel may reach another device: no remote copies, remote signals or barrier semaphores. Data moves between devices by JAX's collectives and lax.ppermute only.
A program may use at most 256 MiB of HBM per device.

```python
import jax
import jax.numpy as jnp
from jax import lax

R = 24576
W = 512
TILE = 384
NT = 64
N_PCOL = 16


def touch_ends(array, stream_key, least, largest):
    spot = [jax.random.randint(jax.random.fold_in(stream_key, axis), (), 0, length) for axis, length in enumerate(array.shape)]
    widest = array.shape.index(max(array.shape))
    beside = spot[:widest] + [(spot[widest] + 1) % array.shape[widest]] + spot[widest + 1:]
    return array.at[tuple(spot)].set(least).at[tuple(beside)].set(largest)


def spiked(values, stream_key, source, target, shards_of, factor):
    owner, partner = [(jnp.arange(values.shape[dim]) // (values.shape[dim] // shards_of)).reshape([-1 if axis == dim else 1 for axis in range(values.ndim)]) for dim in (source, target)]
    chosen = jax.random.permutation(stream_key, shards_of)[partner]
    strong = (owner == chosen) | (owner == (partner + shards_of // 2) % shards_of)
    return jnp.where(strong, factor * values, values)


def block_scale(key, dims, pieces, least, high):
    gain = 1.0
    for position, parts in pieces:
        draws = jax.random.uniform(jax.random.fold_in(jax.random.fold_in(key, 6), position), (parts,), jnp.float32, least / len(pieces), high / len(pieces))
        gain = gain * jnp.repeat(jnp.exp(draws), dims[position] // parts).reshape((-1,) + (1,) * (len(dims) - 1 - position))
    return gain


def gaussian(rng, extent, deviation, reach, cuts=(), kind=jnp.bfloat16):
    entries = deviation * jax.random.normal(rng, extent, jnp.float32)
    if cuts:
        entries = entries * block_scale(rng, extent, cuts, -0.22, 0.18)
    return jnp.clip(entries, -reach, reach).astype(kind)


def heavy_noise(key, extent, deviation, reach, cuts, heavy, kind=jnp.bfloat16):
    result = deviation * jax.random.normal(key, extent, jnp.float32)
    if cuts:
        result = result * block_scale(key, extent, cuts, -0.22, 0.18)
    return jnp.clip(spiked(result, jax.random.fold_in(key, 3), *heavy), -reach, reach).astype(kind)


def setup_inputs(seed: int = 0) -> dict:
    arg_keys = jax.random.split(jax.random.key(seed), 10)
    return {
        "ancestor_inverse": heavy_noise(arg_keys[0], (R, R), 1.0, 6.0, ((0, 2), (1, 16)), (1, 0, 16, 2.0)),
        "tile_pattern": touch_ends((jax.random.randint(arg_keys[1], (NT, NT), 0, 4) < 3).astype(jnp.int32), jax.random.fold_in(arg_keys[1], 1), 0, 1),
        "rows_first": touch_ends((jax.random.randint(arg_keys[2], (R,), 0, 2) < 1).astype(jnp.int32), jax.random.fold_in(arg_keys[2], 1), 0, 1),
        "rows_second": touch_ends((jax.random.randint(arg_keys[3], (R,), 0, 8) < 7).astype(jnp.int32), jax.random.fold_in(arg_keys[3], 1), 0, 1),
        "panel_first": gaussian(arg_keys[4], (R, W), R ** -0.5, 0.0390625, ((0, 2), (1, 16))),
        "panel_second": heavy_noise(arg_keys[5], (R, W), (R // 8) ** -0.5, 0.15625, ((0, 2), (1, 16)), (0, 1, 16, 2.0)),
        "inner_panel": gaussian(arg_keys[6], (W, W), W ** -0.5, 0.25),
        "pivot_first": gaussian(arg_keys[7], (W, W), 1.0, 6.0, (), jnp.float32),
        "pivot_second": gaussian(arg_keys[8], (W, W), 1.0, 6.0, (), jnp.float32),
    }


def mask_tiles(block, pattern, row_start, col_start):
    tile_rows = block.shape[0] // TILE
    tile_cols = block.shape[1] // TILE
    window = lax.dynamic_slice(pattern, (row_start, col_start), (tile_rows, tile_cols)).astype(jnp.bfloat16)
    shaped = block.reshape(tile_rows, TILE, tile_cols, TILE) * window[:, None, :, None]
    return shaped.reshape(block.shape)


def reference(ancestor_inverse, tile_pattern, rows_first, rows_second, panel_first, panel_second, inner_panel, pivot_first, pivot_second):
    struct_first = rows_first.astype(jnp.bfloat16)[:, None]
    struct_second = struct_first * rows_second.astype(jnp.bfloat16)[:, None]
    masked_first = panel_first * struct_first
    masked_second = panel_second * struct_second
    col_block = R // N_PCOL

    def step(carry, index):
        start = (index * col_block).astype(jnp.int32)
        block = lax.dynamic_slice_in_dim(ancestor_inverse, start, col_block, 1)
        block = mask_tiles(block, tile_pattern, jnp.int32(0), (index * (col_block // TILE)).astype(jnp.int32))
        first = lax.dynamic_slice_in_dim(masked_first, start, col_block, 0)
        second = lax.dynamic_slice_in_dim(masked_second, start, col_block, 0)
        term_first = lax.optimization_barrier(jnp.dot(block, first, preferred_element_type=jnp.float32).astype(jnp.bfloat16))
        term_second = lax.optimization_barrier(jnp.dot(block, second, preferred_element_type=jnp.float32).astype(jnp.bfloat16))
        return (carry[0] + term_first.astype(jnp.float32), carry[1] + term_second.astype(jnp.float32)), None

    zeros = jnp.zeros((R, W), jnp.float32)
    (sum_first, sum_second), _ = lax.scan(step, (zeros, zeros), jnp.arange(N_PCOL, dtype=jnp.int32))
    column_first = (-sum_first).astype(jnp.bfloat16)
    diagonal_first = pivot_first - jnp.dot(masked_first.T, column_first, preferred_element_type=jnp.float32)
    column_second = (-(sum_second + jnp.dot(column_first, inner_panel, preferred_element_type=jnp.float32))).astype(jnp.bfloat16)
    inner_wide = inner_panel.astype(jnp.float32)
    crossed = jnp.dot(column_first.T, masked_second, preferred_element_type=jnp.float32)
    inner_second = -(jnp.dot(diagonal_first, inner_wide, precision=lax.Precision.HIGHEST) + crossed)
    diagonal_second = pivot_second - jnp.dot(inner_wide.T, inner_second, precision=lax.Precision.HIGHEST) - jnp.dot(masked_second.T, column_second, preferred_element_type=jnp.float32)
    return column_first, diagonal_first, inner_second, column_second, diagonal_second
```

```python
import functools

import jax
import jax.numpy as jnp
from jax import lax
from jax.experimental import pallas as pl
from jax.experimental.pallas import tpu as pltpu
from jax.sharding import PartitionSpec as P


TILE = 384
BF = jnp.bfloat16
F32 = jnp.float32
BOTH = ("prow", "pcol")


PARAMS = pltpu.CompilerParams(vmem_limit_bytes=67043328)


def whole(*shape):
    return pl.BlockSpec(shape, lambda *_: (0,) * len(shape))


def product_kernel(start, half, count, meta_ref, pattern_ref, *refs):
    inverse_refs, panel_refs, outs = refs[:4], refs[4 : 4 + count], refs[-2 * count :]
    step = start + pl.program_id(0)
    tiles = inverse_refs[0].shape[1] // TILE
    for which, inverse_ref in enumerate(inverse_refs):
        tile_row = meta_ref[step * 4 + which] * half // TILE
        pieces = []
        for tile in range(tiles):
            keep = pattern_ref[tile_row * tiles + tile] != 0
            block = inverse_ref[:, tile * TILE : (tile + 1) * TILE]
            pieces.append(jnp.where(keep, block, jnp.zeros_like(block)))
        kept = jnp.concatenate(pieces, axis=1)
        for number, panel_ref in enumerate(panel_refs):
            product = lax.dot_general(
                kept, panel_ref[...], (((1,), (1,)), ((), ())), preferred_element_type=F32
            )
            outs[number + which // 2 * count][0, which % 2] = product.astype(BF)


def products(start, stop, meta, pattern, inverse, panels, half, after=()):
    width, depth = panels[0].shape
    wide = width * len(panels)
    count = stop - start
    spec = lambda which: pl.BlockSpec(
        (half, depth), lambda i, m, p: (m[(start + i) * 4 + which], 0)
    )
    out = jax.ShapeDtypeStruct((count, 2, half, width), BF)
    out_spec = pl.BlockSpec((1, 2, half, width), lambda i, m, p: (i, 0, 0, 0))
    return pl.pallas_call(
        functools.partial(product_kernel, start, half, len(panels)),
        out_shape=[out] * (2 * len(panels)),
        grid_spec=pltpu.PrefetchScalarGridSpec(
            num_scalar_prefetch=2,
            grid=(count,),
            in_specs=[spec(which) for which in range(4)]
            + [whole(width, depth)] * len(panels)
            + [pl.BlockSpec(memory_space=pl.ANY)] * len(after),
            out_specs=[out_spec] * (2 * len(panels)),
        ),
        cost_estimate=pl.CostEstimate(
            flops=8 * count * half * wide * depth,
            bytes_accessed=2 * (4 * count * half * (depth + wide) + wide * depth),
            transcendentals=0,
        ),
        compiler_params=PARAMS,
        name="products",
    )(meta, pattern, inverse, inverse, inverse, inverse, *panels, *after)


def add_kernel(arrived, last, *refs):
    own_ref, core_ref, outs = refs[0], refs[1], refs[2 + 2 * arrived :]
    for side in range(2):
        total = own_ref[0, side].astype(F32) + core_ref[0, side].astype(F32)
        if arrived:
            total = total + refs[2 + side][...].astype(F32)
        if last:
            outs[0][side] = total
        else:
            outs[side][...] = total.astype(BF)


def add(index, own, core_in, arrived, last):
    _, _, half, width = own.shape
    parts = 2 if half % 32 == 0 else 1
    rows = half // parts
    made = pl.BlockSpec((1, 2, rows, width), lambda i: (index, 0, i, 0))
    moving = pl.BlockSpec((rows, width), lambda i: (i, 0))
    if last:
        out_shape = [jax.ShapeDtypeStruct((2, half, width), F32)]
        out_specs = [pl.BlockSpec((2, rows, width), lambda i: (0, i, 0))]
    else:
        out_shape = [jax.ShapeDtypeStruct((half, width), BF)] * 2
        out_specs = [moving] * 2
    return pl.pallas_call(
        functools.partial(add_kernel, len(arrived) > 0, last),
        out_shape=out_shape,
        grid=(parts,),
        in_specs=[made, made] + [moving] * len(arrived),
        out_specs=out_specs,
        cost_estimate=pl.CostEstimate(
            flops=6 * half * width, bytes_accessed=16 * half * width, transcendentals=0
        ),
        compiler_params=PARAMS,
        name="add",
    )(own, core_in, *arrived)


def stages_of(rows, cols):
    def core(r, c):
        return c % 2, lambda m: (r, c - c % 2 + m)

    def near(r, c):
        return r * 2 + c // 2 % 2, lambda m: (m // 2, c - c % 4 + m % 2 * 2 + c % 2)

    def far(r, c):
        return c // 4, lambda m: (r, m * 4 + c % 4)

    return ((2, core), (rows * 2, near), (cols // 4, far))


def to_follower(value, rows, cols, members, group, shift):
    pairs = []
    for r in range(rows):
        for c in range(cols):
            at, member = group(r, c)
            to_r, to_c = member((at + shift) % members)
            pairs.append((r * cols + c, to_r * cols + to_c))
    return lax.ppermute(value, BOTH, pairs)


def cut_into(outs, total_ref, at):
    size = outs[0].shape[0]
    for place, out in enumerate(outs):
        start = lax.rem(at + place, len(outs)) * size
        if size % 8 == 0:
            start = pl.multiple_of(start, size)
        out[...] = total_ref[pl.ds(start, size), :].astype(BF)


def cut_kernel(members, at_ref, *refs):
    sources, outs = refs[: -members - 1], refs[-members - 1 : -1]
    total = sources[0][...].astype(F32)
    for source in sources[1:]:
        total = total + source[...].astype(F32)
    if members == 1:
        outs[0][...] = total.astype(BF)
    else:
        refs[-1][...] = total
        cut_into(outs, refs[-1], at_ref[0])


def cut(at, members, sources):
    rows, width = sources[0].shape
    size = rows // members
    return pl.pallas_call(
        functools.partial(cut_kernel, members),
        out_shape=[jax.ShapeDtypeStruct((size, width), BF)] * members,
        grid_spec=pltpu.PrefetchScalarGridSpec(
            num_scalar_prefetch=1,
            grid=(1,),
            in_specs=[whole(rows, width)] * len(sources),
            out_specs=[whole(size, width)] * members,
            scratch_shapes=[pltpu.VMEM((rows, width), F32)],
        ),
        compiler_params=PARAMS,
        name="cut",
    )(at[None], *sources)


def place_into(out_ref, pieces, at):
    size = pieces[0].shape[0]
    for place, ref in enumerate(pieces):
        start = lax.rem(at + place, len(pieces)) * size
        if size % 16 == 0:
            start = pl.multiple_of(start, size)
        out_ref[pl.ds(start, size), :] = ref[...].astype(out_ref.dtype)


def place_kernel(at_ref, *refs):
    place_into(refs[-1], refs[:-1], at_ref[0])


def place_all(at, pieces):
    size, width = pieces[0].shape
    shape = (len(pieces) * size, width)
    return pl.pallas_call(
        place_kernel,
        out_shape=jax.ShapeDtypeStruct(shape, BF if size % 16 == 0 else F32),
        grid_spec=pltpu.PrefetchScalarGridSpec(
            num_scalar_prefetch=1,
            grid=(1,),
            in_specs=[whole(size, width)] * len(pieces),
            out_specs=whole(*shape),
        ),
        compiler_params=PARAMS,
        name="place",
    )(at[None], *pieces).astype(BF)


def first_kernel(at_ref, ends_ref, p1_ref, p2_ref, inner_ref, column_ref, lead_ref, *refs):
    width = inner_ref.shape[0]
    column = (-ends_ref[...]).astype(BF)
    column_ref[...] = column
    lead_ref[...] = jnp.dot(column, inner_ref[...], preferred_element_type=F32)
    refs[-1][:width] = jnp.dot(p1_ref[...], column, preferred_element_type=F32)
    refs[-1][width:] = jnp.dot(p2_ref[...], column, preferred_element_type=F32)
    cut_into(refs[:-1], refs[-1], at_ref[0])


def first_column(at, ends, p1, p2, inner):
    share, width = ends.shape
    return pl.pallas_call(
        first_kernel,
        out_shape=[
            jax.ShapeDtypeStruct((share, width), BF),
            jax.ShapeDtypeStruct((share, width), F32),
            jax.ShapeDtypeStruct((width, width), BF),
            jax.ShapeDtypeStruct((width, width), BF),
        ],
        grid_spec=pltpu.PrefetchScalarGridSpec(
            num_scalar_prefetch=1,
            grid=(1,),
            in_specs=[whole(share, width), whole(width, share), whole(width, share), whole(width, width)],
            out_specs=[whole(share, width)] * 2 + [whole(width, width)] * 2,
            scratch_shapes=[pltpu.VMEM((2 * width, width), F32)],
        ),
        compiler_params=PARAMS,
        name="first_column",
    )(at[None], ends, p1, p2, inner)


def second_kernel(at_ref, ends_ref, lead_ref, p2_ref, column_ref, *refs):
    column = (-(ends_ref[...] + lead_ref[...])).astype(BF)
    column_ref[...] = column
    refs[-1][...] = jnp.dot(p2_ref[...], column, preferred_element_type=F32)
    cut_into(refs[:-1], refs[-1], at_ref[0])


def second_column(at, ends, lead, p2):
    share, width = ends.shape
    return pl.pallas_call(
        second_kernel,
        out_shape=[
            jax.ShapeDtypeStruct((share, width), BF),
            jax.ShapeDtypeStruct((width // 2, width), BF),
            jax.ShapeDtypeStruct((width // 2, width), BF),
        ],
        grid_spec=pltpu.PrefetchScalarGridSpec(
            num_scalar_prefetch=1,
            grid=(1,),
            in_specs=[whole(share, width), whole(share, width), whole(width, share)],
            out_specs=[whole(share, width)] + [whole(width // 2, width)] * 2,
            scratch_shapes=[pltpu.VMEM((width, width), F32)],
        ),
        compiler_params=PARAMS,
        name="second_column",
    )(at[None], ends, lead, p2)


def sharp(left, right):
    high = left.astype(BF)
    rest = left - high.astype(F32)
    middle = rest.astype(BF)
    low = (rest - middle.astype(F32)).astype(BF)
    dot = lambda part: jnp.dot(part, right, preferred_element_type=F32)
    return dot(low) + dot(middle) + dot(high)


def close_kernel(at_ref, low_ref, high_ref, first_ref, second_ref, inner_ref, *refs):
    diagonal_ref, cross_ref, base_ref, sums_ref = refs
    place_into(sums_ref, (low_ref, high_ref), at_ref[0])
    width = inner_ref.shape[0]
    diagonal = first_ref[...] - sums_ref[:width]
    diagonal_ref[...] = diagonal
    cross = -(sharp(diagonal, inner_ref[...]) + sums_ref[width:].T)
    cross_ref[...] = cross
    base_ref[...] = second_ref[...] - sharp(cross.T, inner_ref[...]).T


def close(at, pieces, pivot_first, pivot_second, inner_panel):
    width = inner_panel.shape[0]
    square = whole(width, width)
    return pl.pallas_call(
        close_kernel,
        out_shape=[jax.ShapeDtypeStruct((width, width), F32)] * 3,
        grid_spec=pltpu.PrefetchScalarGridSpec(
            num_scalar_prefetch=1,
            grid=(1,),
            in_specs=[square] * 5,
            out_specs=[square] * 3,
            scratch_shapes=[pltpu.VMEM((2 * width, width), F32)],
        ),
        compiler_params=PARAMS,
        name="close",
    )(at[None], *pieces, pivot_first, pivot_second, inner_panel)


def last_kernel(at_ref, low_ref, high_ref, base_ref, out_ref):
    place_into(out_ref, (low_ref, high_ref), at_ref[0])
    out_ref[...] = base_ref[...] - out_ref[...]


def last(at, pieces, base):
    width = base.shape[0]
    part = whole(width // 2, width)
    return pl.pallas_call(
        last_kernel,
        out_shape=jax.ShapeDtypeStruct((width, width), F32),
        grid_spec=pltpu.PrefetchScalarGridSpec(
            num_scalar_prefetch=1,
            grid=(1,),
            in_specs=[part, part, whole(width, width)],
            out_specs=whole(width, width),
        ),
        compiler_params=PARAMS,
        name="last",
    )(at[None], *pieces, base)


def plan(chips):
    make = lambda rings, start, stop: ("make", rings, start, min(stop, chips))
    step = lambda kind, ring, at: (kind, (ring,), at, at + 1)
    events = [make((0,), 0, 1), step("add", 0, 0), make((0,), 1, 3), step("add", 0, 1)]
    events += [make((0,), 3, 4), step("add", 0, 2), make((1,), 0, 4), step("add", 1, 0)]
    made = 4
    for at in range(3, chips):
        events.append(step("add", 0, at))
        if made < chips:
            events.append(make((0, 1), made, made + 2))
            made += 2
        events.append(step("add", 1, at - 2))
    events += [step("sum", 0, 0), step("add", 1, chips - 2), step("sum", 0, 1)]
    events += [step("add", 1, chips - 1), step("sum", 1, 0), step("sum", 0, 2)]
    for at in range(1, 6):
        events.append(step("sum", 1, at))
        if at < 4:
            events.append(step("sum", 0, at + 2))
    return events


def body(
    ancestor_inverse,
    tile_pattern,
    rows_first,
    rows_second,
    panel_first,
    panel_second,
    inner_panel,
    pivot_first,
    pivot_second,
):
    rows, cols = lax.axis_size("prow"), lax.axis_size("pcol")
    row_id, col_id = lax.axis_index("prow"), lax.axis_index("pcol")
    row_block, col_block = ancestor_inverse.shape
    share = row_block // cols
    half = share // 2
    width = inner_panel.shape[0]
    local = panel_first.shape[1]
    piece = local // rows
    chips = cols // 2

    tile_rows, tile_cols = row_block // TILE, col_block // TILE
    pattern = lax.dynamic_slice(
        tile_pattern, (row_id * tile_rows, col_id * tile_cols), (tile_rows, tile_cols)
    ).reshape(-1)
    chip, core = col_id // 2, col_id % 2
    place = jnp.where(chip % 2 == 0, chip // 2, chips - 1 - chip // 2)
    steps = jnp.arange(chips, dtype=jnp.int32)
    dest = jnp.stack([(place - 1 - steps) % chips, (place + 1 + steps) % chips], axis=1)
    dest = jnp.where(dest < chips // 2, 2 * dest, 2 * (chips - 1 - dest) + 1)
    side = jnp.arange(2, dtype=jnp.int32)[None, :]
    meta = jnp.concatenate(
        [(dest * 2 + core) * 2 + side, (dest * 2 + 1 - core) * 2 + side], axis=1
    ).reshape(-1)
    order = [2 * i if i < chips // 2 else 2 * (chips - 1 - i) + 1 for i in range(chips)]
    onward = [
        (order[i] * 2 + k, order[(i + 1) % chips] * 2 + k) for i in range(chips) for k in range(2)
    ]
    backward = [(b, a) for a, b in onward]
    swap = [(c, c ^ 1) for c in range(cols)]
    to_share = [
        (a * cols + k, k * rows + (a + 1) % rows) for a in range(rows) for k in range(cols)
    ]

    struct_first = lax.dynamic_slice_in_dim(rows_first, row_id * row_block, row_block).astype(BF)
    struct_second = struct_first * lax.dynamic_slice_in_dim(
        rows_second, row_id * row_block, row_block
    ).astype(BF)

    def spread(panel, struct):
        turned = (panel.T * struct[None, :]).reshape(rows, piece, row_block)
        gathered = jnp.zeros((rows, cols // rows, piece, col_block), BF)
        for shift in range(rows):
            part = lax.dynamic_index_in_dim(turned, (row_id + shift) % rows, 0, keepdims=False)
            if shift:
                part = lax.ppermute(part, "prow", [(a, (a + shift) % rows) for a in range(rows)])
            part = part.reshape(piece, cols // rows, col_block).transpose(1, 0, 2)
            gathered = lax.dynamic_update_index_in_dim(gathered, part, (row_id - shift) % rows, 0)
        return gathered.reshape(cols, piece, col_block)

    def exchange(gathered):
        return lax.all_to_all(gathered, "pcol", 0, 0, tiled=True)

    def complete(mine):
        full = jnp.zeros((cols, rows, piece, col_block), BF)
        for shift in range(rows):
            part = mine
            if shift:
                part = lax.ppermute(part, "prow", [(a, (a - shift) % rows) for a in range(rows)])
            full = lax.dynamic_update_index_in_dim(full, part, (row_id + shift) % rows, 1)
        return full.reshape(width, col_block)

    gathered = [spread(panel_first, struct_first), spread(panel_second, struct_second)]
    mine_first = exchange(gathered[0])
    mine_second = exchange(gathered[1])
    panels = [complete(mine_first)]
    panels.append(complete(mine_second))

    own_rows = []
    for number, panel in enumerate(panels):
        own_rows.append(
            lax.ppermute(
                lax.dynamic_slice_in_dim(panel, (row_id + 1) % rows * share, share, 1),
                BOTH,
                to_share,
            )
        )

    made, arrived, ends, summed = [[], []], [[], []], [None, None], [None, None]
    places = (col_id % 2, row_id * 2 + (col_id // 2) % 2, col_id // 4)
    stages = list(zip(stages_of(rows, cols), places))
    for event in plan(chips):
        kind, rings, start, stop = event
        if kind == "make":
            made_now = products(
                start,
                stop,
                meta,
                pattern,
                ancestor_inverse,
                [panels[r] for r in rings],
                half,
                (mine_second,) if rings == (0,) and start == 1 else (),
            )
            theirs = [lax.ppermute(p, "pcol", swap) for p in made_now[len(rings) :]]
            for column, ring in enumerate(rings):
                made[ring] += [(i, made_now[column], theirs[column]) for i in range(stop - start)]
        elif kind == "add":
            ring = rings[0]
            total = add(*made[ring][start], arrived[ring], start == chips - 1)
            if start == chips - 1:
                ends[ring] = total[0].reshape(share, width)
            else:
                arrived[ring] = [
                    lax.ppermute(total[0], "pcol", onward),
                    lax.ppermute(total[1], "pcol", backward),
                ]
        else:
            ring, number = rings[0], start
            (members, group), at = stages[min(number, 5 - number)]
            if number == 0 and ring == 0:
                column_first, lead, *cuts = first_column(at, ends[0], *own_rows, inner_panel)
            elif number == 0:
                column_second, *cuts = second_column(at, ends[1], lead, own_rows[1])
            elif number == 1:
                cuts = cut(at, members, summed[ring])
            elif number < 4:
                cuts = cut(at, 1, summed[ring])
            elif number == 4:
                cuts = [place_all(stages[1][1], summed[ring])]
            elif ring == 0:
                diagonal_first, inner_second, base = close(
                    at, summed[0], pivot_first, pivot_second, inner_panel
                )
            else:
                diagonal_second = last(at, summed[1], base)
            if number < 5:
                (members, group), _ = stages[(0, 1, 2, 1, 0)[number]]
                summed[ring] = [cuts[0]] + [
                    to_follower(
                        cuts[shift] if number < 2 else cuts[0],
                        rows,
                        cols,
                        members,
                        group,
                        shift if number < 2 else members - shift,
                    )
                    for shift in range(1, members)
                ]
    return (column_first, diagonal_first, inner_second, column_second, diagonal_second)


def solution(mesh):
    return jax.shard_map(
        body,
        mesh=mesh,
        in_specs=(
            P("prow", "pcol"),
            P(),
            P(),
            P(),
            P("prow", "pcol"),
            P("prow", "pcol"),
            P(),
            P(),
            P(),
        ),
        out_specs=(P(("prow", "pcol"), None), P(), P(), P(("prow", "pcol"), None), P()),
        check_vma=False,
    )
```

```python
import functools

import jax
import jax.numpy as jnp
from jax import lax
from jax.experimental import pallas as pl
from jax.experimental.pallas import tpu as pltpu
from jax.sharding import PartitionSpec as P


TILE = 384
BF = jnp.bfloat16
F32 = jnp.float32
BOTH = ("prow", "pcol")


PARAMS = pltpu.CompilerParams(vmem_limit_bytes=67043328)


def whole(*shape):
    return pl.BlockSpec(shape, lambda *_: (0,) * len(shape))


def product_kernel(start, half, count, meta_ref, pattern_ref, *refs):
    inverse_refs, panel_refs, outs = refs[:4], refs[4 : 4 + count], refs[-2 * count :]
    step = start + pl.program_id(0)
    tiles = inverse_refs[0].shape[1] // TILE
    for which, inverse_ref in enumerate(inverse_refs):
        tile_row = meta_ref[step * 4 + which] * half // TILE
        pieces = []
        for tile in range(tiles):
            keep = pattern_ref[tile_row * tiles + tile] != 0
            block = inverse_ref[:, tile * TILE : (tile + 1) * TILE]
            pieces.append(jnp.where(keep, block, jnp.zeros_like(block)))
        kept = jnp.concatenate(pieces, axis=1)
        for number, panel_ref in enumerate(panel_refs):
            product = lax.dot_general(
                kept, panel_ref[...], (((1,), (1,)), ((), ())), preferred_element_type=F32
            )
            outs[number + which // 2 * count][0, which % 2] = product.astype(BF)


def products(start, stop, meta, pattern, inverse, panels, half, after=()):
    width, depth = panels[0].shape
    wide = width * len(panels)
    count = stop - start
    spec = lambda which: pl.BlockSpec(
        (half, depth), lambda i, m, p: (m[(start + i) * 4 + which], 0)
    )
    out = jax.ShapeDtypeStruct((count, 2, half, width), BF)
    out_spec = pl.BlockSpec((1, 2, half, width), lambda i, m, p: (i, 0, 0, 0))
    return pl.pallas_call(
        functools.partial(product_kernel, start, half, len(panels)),
        out_shape=[out] * (2 * len(panels)),
        grid_spec=pltpu.PrefetchScalarGridSpec(
            num_scalar_prefetch=2,
            grid=(count,),
            in_specs=[spec(which) for which in range(4)]
            + [whole(width, depth)] * len(panels)
            + [pl.BlockSpec(memory_space=pl.ANY)] * len(after),
            out_specs=[out_spec] * (2 * len(panels)),
        ),
        cost_estimate=pl.CostEstimate(
            flops=8 * count * half * wide * depth,
            bytes_accessed=2 * (4 * count * half * (depth + wide) + wide * depth),
            transcendentals=0,
        ),
        compiler_params=PARAMS,
        name="products",
    )(meta, pattern, inverse, inverse, inverse, inverse, *panels, *after)


def add_kernel(arrived, last, *refs):
    own_ref, core_ref, outs = refs[0], refs[1], refs[2 + 2 * arrived :]
    for side in range(2):
        total = own_ref[0, side].astype(F32) + core_ref[0, side].astype(F32)
        if arrived:
            total = total + refs[2 + side][...].astype(F32)
        if last:
            outs[0][side] = total
        else:
            outs[side][...] = total.astype(BF)


def add(index, own, core_in, arrived, last):
    _, _, half, width = own.shape
    parts = 2 if half % 32 == 0 else 1
    rows = half // parts
    made = pl.BlockSpec((1, 2, rows, width), lambda i: (index, 0, i, 0))
    moving = pl.BlockSpec((rows, width), lambda i: (i, 0))
    if last:
        out_shape = [jax.ShapeDtypeStruct((2, half, width), F32)]
        out_specs = [pl.BlockSpec((2, rows, width), lambda i: (0, i, 0))]
    else:
        out_shape = [jax.ShapeDtypeStruct((half, width), BF)] * 2
        out_specs = [moving] * 2
    return pl.pallas_call(
        functools.partial(add_kernel, len(arrived) > 0, last),
        out_shape=out_shape,
        grid=(parts,),
        in_specs=[made, made] + [moving] * len(arrived),
        out_specs=out_specs,
        cost_estimate=pl.CostEstimate(
            flops=6 * half * width, bytes_accessed=16 * half * width, transcendentals=0
        ),
        compiler_params=PARAMS,
        name="add",
    )(own, core_in, *arrived)


def stages_of(rows, cols):
    def core(r, c):
        return c % 2, lambda m: (r, c - c % 2 + m)

    def near(r, c):
        return r * 2 + c // 2 % 2, lambda m: (m // 2, c - c % 4 + m % 2 * 2 + c % 2)

    def far(r, c):
        return c // 4, lambda m: (r, m * 4 + c % 4)

    return ((2, core), (rows * 2, near), (cols // 4, far))


def to_follower(value, rows, cols, members, group, shift):
    pairs = []
    for r in range(rows):
        for c in range(cols):
            at, member = group(r, c)
            to_r, to_c = member((at + shift) % members)
            pairs.append((r * cols + c, to_r * cols + to_c))
    return lax.ppermute(value, BOTH, pairs)


def cut_into(outs, total_ref, at):
    size = outs[0].shape[0]
    for place, out in enumerate(outs):
        start = lax.rem(at + place, len(outs)) * size
        if size % 8 == 0:
            start = pl.multiple_of(start, size)
        out[...] = total_ref[pl.ds(start, size), :].astype(BF)


def cut_kernel(members, at_ref, *refs):
    sources, outs = refs[: -members - 1], refs[-members - 1 : -1]
    total = sources[0][...].astype(F32)
    for source in sources[1:]:
        total = total + source[...].astype(F32)
    if members == 1:
        outs[0][...] = total.astype(BF)
    else:
        refs[-1][...] = total
        cut_into(outs, refs[-1], at_ref[0])


def cut(at, members, sources):
    rows, width = sources[0].shape
    size = rows // members
    return pl.pallas_call(
        functools.partial(cut_kernel, members),
        out_shape=[jax.ShapeDtypeStruct((size, width), BF)] * members,
        grid_spec=pltpu.PrefetchScalarGridSpec(
            num_scalar_prefetch=1,
            grid=(1,),
            in_specs=[whole(rows, width)] * len(sources),
            out_specs=[whole(size, width)] * members,
            scratch_shapes=[pltpu.VMEM((rows, width), F32)],
        ),
        compiler_params=PARAMS,
        name="cut",
    )(at[None], *sources)


def place_into(out_ref, pieces, at):
    size = pieces[0].shape[0]
    for place, ref in enumerate(pieces):
        start = lax.rem(at + place, len(pieces)) * size
        if size % 16 == 0:
            start = pl.multiple_of(start, size)
        out_ref[pl.ds(start, size), :] = ref[...].astype(out_ref.dtype)


def place_kernel(at_ref, *refs):
    place_into(refs[-1], refs[:-1], at_ref[0])


def place_all(at, pieces):
    size, width = pieces[0].shape
    shape = (len(pieces) * size, width)
    return pl.pallas_call(
        place_kernel,
        out_shape=jax.ShapeDtypeStruct(shape, BF if size % 16 == 0 else F32),
        grid_spec=pltpu.PrefetchScalarGridSpec(
            num_scalar_prefetch=1,
            grid=(1,),
            in_specs=[whole(size, width)] * len(pieces),
            out_specs=whole(*shape),
        ),
        compiler_params=PARAMS,
        name="place",
    )(at[None], *pieces).astype(BF)


def first_kernel(at_ref, ends_ref, p1_ref, p2_ref, inner_ref, column_ref, lead_ref, *refs):
    width = inner_ref.shape[0]
    column = (-ends_ref[...]).astype(BF)
    column_ref[...] = column
    lead_ref[...] = jnp.dot(column, inner_ref[...], preferred_element_type=F32)
    refs[-1][:width] = jnp.dot(p1_ref[...], column, preferred_element_type=F32)
    refs[-1][width:] = jnp.dot(p2_ref[...], column, preferred_element_type=F32)
    cut_into(refs[:-1], refs[-1], at_ref[0])


def first_column(at, ends, p1, p2, inner):
    share, width = ends.shape
    return pl.pallas_call(
        first_kernel,
        out_shape=[
            jax.ShapeDtypeStruct((share, width), BF),
            jax.ShapeDtypeStruct((share, width), F32),
            jax.ShapeDtypeStruct((width, width), BF),
            jax.ShapeDtypeStruct((width, width), BF),
        ],
        grid_spec=pltpu.PrefetchScalarGridSpec(
            num_scalar_prefetch=1,
            grid=(1,),
            in_specs=[whole(share, width), whole(width, share), whole(width, share), whole(width, width)],
            out_specs=[whole(share, width)] * 2 + [whole(width, width)] * 2,
            scratch_shapes=[pltpu.VMEM((2 * width, width), F32)],
        ),
        compiler_params=PARAMS,
        name="first_column",
    )(at[None], ends, p1, p2, inner)


def second_kernel(at_ref, ends_ref, lead_ref, p2_ref, column_ref, *refs):
    column = (-(ends_ref[...] + lead_ref[...])).astype(BF)
    column_ref[...] = column
    refs[-1][...] = jnp.dot(p2_ref[...], column, preferred_element_type=F32)
    cut_into(refs[:-1], refs[-1], at_ref[0])


def second_column(at, ends, lead, p2):
    share, width = ends.shape
    return pl.pallas_call(
        second_kernel,
        out_shape=[
            jax.ShapeDtypeStruct((share, width), BF),
            jax.ShapeDtypeStruct((width // 2, width), BF),
            jax.ShapeDtypeStruct((width // 2, width), BF),
        ],
        grid_spec=pltpu.PrefetchScalarGridSpec(
            num_scalar_prefetch=1,
            grid=(1,),
            in_specs=[whole(share, width), whole(share, width), whole(width, share)],
            out_specs=[whole(share, width)] + [whole(width // 2, width)] * 2,
            scratch_shapes=[pltpu.VMEM((width, width), F32)],
        ),
        compiler_params=PARAMS,
        name="second_column",
    )(at[None], ends, lead, p2)


def sharp(left, right):
    high = left.astype(BF)
    rest = left - high.astype(F32)
    middle = rest.astype(BF)
    low = (rest - middle.astype(F32)).astype(BF)
    dot = lambda part: jnp.dot(part, right, preferred_element_type=F32)
    return dot(low) + dot(middle) + dot(high)


def close_kernel(at_ref, low_ref, high_ref, first_ref, second_ref, inner_ref, *refs):
    diagonal_ref, cross_ref, base_ref, sums_ref = refs
    place_into(sums_ref, (low_ref, high_ref), at_ref[0])
    width = inner_ref.shape[0]
    diagonal = first_ref[...] - sums_ref[:width]
    diagonal_ref[...] = diagonal
    cross = -(sharp(diagonal, inner_ref[...]) + sums_ref[width:].T)
    cross_ref[...] = cross
    base_ref[...] = second_ref[...] - sharp(cross.T, inner_ref[...]).T


def close(at, pieces, pivot_first, pivot_second, inner_panel):
    width = inner_panel.shape[0]
    square = whole(width, width)
    return pl.pallas_call(
        close_kernel,
        out_shape=[jax.ShapeDtypeStruct((width, width), F32)] * 3,
        grid_spec=pltpu.PrefetchScalarGridSpec(
            num_scalar_prefetch=1,
            grid=(1,),
            in_specs=[square] * 5,
            out_specs=[square] * 3,
            scratch_shapes=[pltpu.VMEM((2 * width, width), F32)],
        ),
        compiler_params=PARAMS,
        name="close",
    )(at[None], *pieces, pivot_first, pivot_second, inner_panel)


def last_kernel(at_ref, low_ref, high_ref, base_ref, out_ref):
    place_into(out_ref, (low_ref, high_ref), at_ref[0])
    out_ref[...] = base_ref[...] - out_ref[...]


def last(at, pieces, base):
    width = base.shape[0]
    part = whole(width // 2, width)
    return pl.pallas_call(
        last_kernel,
        out_shape=jax.ShapeDtypeStruct((width, width), F32),
        grid_spec=pltpu.PrefetchScalarGridSpec(
            num_scalar_prefetch=1,
            grid=(1,),
            in_specs=[part, part, whole(width, width)],
            out_specs=whole(width, width),
        ),
        compiler_params=PARAMS,
        name="last",
    )(at[None], *pieces, base)


def plan(chips):
    make = lambda rings, start, stop: ("make", rings, start, min(stop, chips))
    step = lambda kind, ring, at: (kind, (ring,), at, at + 1)
    events = [make((0,), 0, 1), step("add", 0, 0), make((0,), 1, 3), step("add", 0, 1)]
    events += [make((1,), 0, 3), step("add", 0, 2), step("add", 1, 0)]
    for at in range(3, chips):
        events += [make((0, 1), at, at + 1), step("add", 1, at - 2), step("add", 0, at)]
    events += [step("sum", 0, 0), step("add", 1, chips - 2), step("sum", 0, 1)]
    events += [step("add", 1, chips - 1), step("sum", 1, 0), step("sum", 0, 2)]
    for at in range(1, 6):
        events.append(step("sum", 1, at))
        if at < 4:
            events.append(step("sum", 0, at + 2))
    return events


def body(
    ancestor_inverse,
    tile_pattern,
    rows_first,
    rows_second,
    panel_first,
    panel_second,
    inner_panel,
    pivot_first,
    pivot_second,
):
    rows, cols = lax.axis_size("prow"), lax.axis_size("pcol")
    row_id, col_id = lax.axis_index("prow"), lax.axis_index("pcol")
    row_block, col_block = ancestor_inverse.shape
    share = row_block // cols
    half = share // 2
    width = inner_panel.shape[0]
    local = panel_first.shape[1]
    piece = local // rows
    chips = cols // 2

    tile_rows, tile_cols = row_block // TILE, col_block // TILE
    pattern = lax.dynamic_slice(
        tile_pattern, (row_id * tile_rows, col_id * tile_cols), (tile_rows, tile_cols)
    ).reshape(-1)
    chip, core = col_id // 2, col_id % 2
    place = jnp.where(chip % 2 == 0, chip // 2, chips - 1 - chip // 2)
    steps = jnp.arange(chips, dtype=jnp.int32)
    dest = jnp.stack([(place - 1 - steps) % chips, (place + 1 + steps) % chips], axis=1)
    dest = jnp.where(dest < chips // 2, 2 * dest, 2 * (chips - 1 - dest) + 1)
    side = jnp.arange(2, dtype=jnp.int32)[None, :]
    meta = jnp.concatenate(
        [(dest * 2 + core) * 2 + side, (dest * 2 + 1 - core) * 2 + side], axis=1
    ).reshape(-1)
    order = [2 * i if i < chips // 2 else 2 * (chips - 1 - i) + 1 for i in range(chips)]
    onward = [
        (order[i] * 2 + k, order[(i + 1) % chips] * 2 + k) for i in range(chips) for k in range(2)
    ]
    backward = [(b, a) for a, b in onward]
    swap = [(c, c ^ 1) for c in range(cols)]
    to_share = [
        (a * cols + k, k * rows + (a + 1) % rows) for a in range(rows) for k in range(cols)
    ]

    struct_first = lax.dynamic_slice_in_dim(rows_first, row_id * row_block, row_block).astype(BF)
    struct_second = struct_first * lax.dynamic_slice_in_dim(
        rows_second, row_id * row_block, row_block
    ).astype(BF)

    def spread(panel, struct):
        turned = (panel.T * struct[None, :]).reshape(rows, piece, row_block)
        gathered = jnp.zeros((rows, cols // rows, piece, col_block), BF)
        for shift in range(rows):
            part = lax.dynamic_index_in_dim(turned, (row_id + shift) % rows, 0, keepdims=False)
            if shift:
                part = lax.ppermute(part, "prow", [(a, (a + shift) % rows) for a in range(rows)])
            part = part.reshape(piece, cols // rows, col_block).transpose(1, 0, 2)
            gathered = lax.dynamic_update_index_in_dim(gathered, part, (row_id - shift) % rows, 0)
        return gathered.reshape(cols, piece, col_block)

    def exchange(gathered):
        return lax.all_to_all(gathered, "pcol", 0, 0, tiled=True)

    def complete(mine):
        full = jnp.zeros((cols, rows, piece, col_block), BF)
        for shift in range(rows):
            part = mine
            if shift:
                part = lax.ppermute(part, "prow", [(a, (a - shift) % rows) for a in range(rows)])
            full = lax.dynamic_update_index_in_dim(full, part, (row_id + shift) % rows, 1)
        return full.reshape(width, col_block)

    gathered = [spread(panel_first, struct_first), spread(panel_second, struct_second)]
    mine_first = exchange(gathered[0])
    mine_second = exchange(gathered[1])
    panels = [complete(mine_first)]
    panels.append(complete(mine_second))

    own_rows = []
    for number, panel in enumerate(panels):
        own_rows.append(
            lax.ppermute(
                lax.dynamic_slice_in_dim(panel, (row_id + 1) % rows * share, share, 1),
                BOTH,
                to_share,
            )
        )

    made, arrived, ends, summed = [[], []], [[], []], [None, None], [None, None]
    places = (col_id % 2, row_id * 2 + (col_id // 2) % 2, col_id // 4)
    stages = list(zip(stages_of(rows, cols), places))
    for event in plan(chips):
        kind, rings, start, stop = event
        if kind == "make":
            made_now = products(
                start,
                stop,
                meta,
                pattern,
                ancestor_inverse,
                [panels[r] for r in rings],
                half,
                (mine_second,) if rings == (0,) and start == 1 else (),
            )
            theirs = [lax.ppermute(p, "pcol", swap) for p in made_now[len(rings) :]]
            for column, ring in enumerate(rings):
                made[ring] += [(i, made_now[column], theirs[column]) for i in range(stop - start)]
        elif kind == "add":
            ring = rings[0]
            total = add(*made[ring][start], arrived[ring], start == chips - 1)
            if start == chips - 1:
                ends[ring] = total[0].reshape(share, width)
            else:
                arrived[ring] = [
                    lax.ppermute(total[0], "pcol", onward),
                    lax.ppermute(total[1], "pcol", backward),
                ]
        else:
            ring, number = rings[0], start
            (members, group), at = stages[min(number, 5 - number)]
            if number == 0 and ring == 0:
                column_first, lead, *cuts = first_column(at, ends[0], *own_rows, inner_panel)
            elif number == 0:
                column_second, *cuts = second_column(at, ends[1], lead, own_rows[1])
            elif number == 1:
                cuts = cut(at, members, summed[ring])
            elif number < 4:
                cuts = cut(at, 1, summed[ring])
            elif number == 4:
                cuts = [place_all(stages[1][1], summed[ring])]
            elif ring == 0:
                diagonal_first, inner_second, base = close(
                    at, summed[0], pivot_first, pivot_second, inner_panel
                )
            else:
                diagonal_second = last(at, summed[1], base)
            if number < 5:
                (members, group), _ = stages[(0, 1, 2, 1, 0)[number]]
                summed[ring] = [cuts[0]] + [
                    to_follower(
                        cuts[shift] if number < 2 else cuts[0],
                        rows,
                        cols,
                        members,
                        group,
                        shift if number < 2 else members - shift,
                    )
                    for shift in range(1, members)
                ]
    return (column_first, diagonal_first, inner_second, column_second, diagonal_second)


def solution(mesh):
    return jax.shard_map(
        body,
        mesh=mesh,
        in_specs=(
            P("prow", "pcol"),
            P(),
            P(),
            P(),
            P("prow", "pcol"),
            P("prow", "pcol"),
            P(),
            P(),
            P(),
        ),
        out_specs=(P(("prow", "pcol"), None), P(), P(), P(("prow", "pcol"), None), P()),
        check_vma=False,
    )
```

```python
import functools

import jax
import jax.numpy as jnp
from jax import lax
from jax.experimental import pallas as pl
from jax.experimental.pallas import tpu as pltpu
from jax.sharding import PartitionSpec as P


TILE = 384
BF = jnp.bfloat16
F32 = jnp.float32
BOTH = ("prow", "pcol")


PARAMS = pltpu.CompilerParams(vmem_limit_bytes=67043328)


def whole(*shape):
    return pl.BlockSpec(shape, lambda *_: (0,) * len(shape))


def product_kernel(start, half, count, meta_ref, pattern_ref, *refs):
    inverse_refs, panel_refs, outs = refs[:4], refs[4 : 4 + count], refs[-2 * count :]
    step = start + pl.program_id(0)
    tiles = inverse_refs[0].shape[1] // TILE
    for which, inverse_ref in enumerate(inverse_refs):
        tile_row = meta_ref[step * 4 + which] * half // TILE
        pieces = []
        for tile in range(tiles):
            keep = pattern_ref[tile_row * tiles + tile] != 0
            block = inverse_ref[:, tile * TILE : (tile + 1) * TILE]
            pieces.append(jnp.where(keep, block, jnp.zeros_like(block)))
        kept = jnp.concatenate(pieces, axis=1)
        for number, panel_ref in enumerate(panel_refs):
            product = lax.dot_general(
                kept, panel_ref[...], (((1,), (1,)), ((), ())), preferred_element_type=F32
            )
            outs[number + which // 2 * count][0, which % 2] = product.astype(BF)


def products(start, stop, meta, pattern, inverse, panels, half, after=()):
    width, depth = panels[0].shape
    wide = width * len(panels)
    count = stop - start
    spec = lambda which: pl.BlockSpec(
        (half, depth), lambda i, m, p: (m[(start + i) * 4 + which], 0)
    )
    out = jax.ShapeDtypeStruct((count, 2, half, width), BF)
    out_spec = pl.BlockSpec((1, 2, half, width), lambda i, m, p: (i, 0, 0, 0))
    return pl.pallas_call(
        functools.partial(product_kernel, start, half, len(panels)),
        out_shape=[out] * (2 * len(panels)),
        grid_spec=pltpu.PrefetchScalarGridSpec(
            num_scalar_prefetch=2,
            grid=(count,),
            in_specs=[spec(which) for which in range(4)]
            + [whole(width, depth)] * len(panels)
            + [pl.BlockSpec(memory_space=pl.ANY)] * len(after),
            out_specs=[out_spec] * (2 * len(panels)),
        ),
        cost_estimate=pl.CostEstimate(
            flops=8 * count * half * wide * depth,
            bytes_accessed=2 * (4 * count * half * (depth + wide) + wide * depth),
            transcendentals=0,
        ),
        compiler_params=PARAMS,
        name="products",
    )(meta, pattern, inverse, inverse, inverse, inverse, *panels, *after)


def add_kernel(arrived, last, *refs):
    own_ref, core_ref, outs = refs[0], refs[1], refs[2 + 2 * arrived :]
    for side in range(2):
        total = own_ref[0, side].astype(F32) + core_ref[0, side].astype(F32)
        if arrived:
            total = total + refs[2 + side][...].astype(F32)
        if last:
            outs[0][side] = total
        else:
            outs[side][...] = total.astype(BF)


def add(index, own, core_in, arrived, last):
    _, _, half, width = own.shape
    parts = 2 if half % 32 == 0 else 1
    rows = half // parts
    made = pl.BlockSpec((1, 2, rows, width), lambda i: (index, 0, i, 0))
    moving = pl.BlockSpec((rows, width), lambda i: (i, 0))
    if last:
        out_shape = [jax.ShapeDtypeStruct((2, half, width), F32)]
        out_specs = [pl.BlockSpec((2, rows, width), lambda i: (0, i, 0))]
    else:
        out_shape = [jax.ShapeDtypeStruct((half, width), BF)] * 2
        out_specs = [moving] * 2
    return pl.pallas_call(
        functools.partial(add_kernel, len(arrived) > 0, last),
        out_shape=out_shape,
        grid=(parts,),
        in_specs=[made, made] + [moving] * len(arrived),
        out_specs=out_specs,
        cost_estimate=pl.CostEstimate(
            flops=6 * half * width, bytes_accessed=16 * half * width, transcendentals=0
        ),
        compiler_params=PARAMS,
        name="add",
    )(own, core_in, *arrived)


def stages_of(rows, cols):
    def core(r, c):
        return c % 2, lambda m: (r, c - c % 2 + m)

    def near(r, c):
        return r * 2 + c // 2 % 2, lambda m: (m // 2, c - c % 4 + m % 2 * 2 + c % 2)

    def far(r, c):
        return c // 4, lambda m: (r, m * 4 + c % 4)

    return ((2, core), (rows * 2, near), (cols // 4, far))


def to_follower(value, rows, cols, members, group, shift):
    pairs = []
    for r in range(rows):
        for c in range(cols):
            at, member = group(r, c)
            to_r, to_c = member((at + shift) % members)
            pairs.append((r * cols + c, to_r * cols + to_c))
    return lax.ppermute(value, BOTH, pairs)


def cut_into(outs, total_ref, at):
    size = outs[0].shape[0]
    for place, out in enumerate(outs):
        start = lax.rem(at + place, len(outs)) * size
        if size % 8 == 0:
            start = pl.multiple_of(start, size)
        out[...] = total_ref[pl.ds(start, size), :].astype(BF)


def cut_kernel(members, at_ref, *refs):
    sources, outs = refs[: -members - 1], refs[-members - 1 : -1]
    total = sources[0][...].astype(F32)
    for source in sources[1:]:
        total = total + source[...].astype(F32)
    if members == 1:
        outs[0][...] = total.astype(BF)
    else:
        refs[-1][...] = total
        cut_into(outs, refs[-1], at_ref[0])


def cut(at, members, sources):
    rows, width = sources[0].shape
    size = rows // members
    return pl.pallas_call(
        functools.partial(cut_kernel, members),
        out_shape=[jax.ShapeDtypeStruct((size, width), BF)] * members,
        grid_spec=pltpu.PrefetchScalarGridSpec(
            num_scalar_prefetch=1,
            grid=(1,),
            in_specs=[whole(rows, width)] * len(sources),
            out_specs=[whole(size, width)] * members,
            scratch_shapes=[pltpu.VMEM((rows, width), F32)],
        ),
        compiler_params=PARAMS,
        name="cut",
    )(at[None], *sources)


def place_into(out_ref, pieces, at):
    size = pieces[0].shape[0]
    for place, ref in enumerate(pieces):
        start = lax.rem(at + place, len(pieces)) * size
        if size % 16 == 0:
            start = pl.multiple_of(start, size)
        out_ref[pl.ds(start, size), :] = ref[...].astype(out_ref.dtype)


def place_kernel(at_ref, *refs):
    place_into(refs[-1], refs[:-1], at_ref[0])


def place_all(at, pieces):
    size, width = pieces[0].shape
    shape = (len(pieces) * size, width)
    return pl.pallas_call(
        place_kernel,
        out_shape=jax.ShapeDtypeStruct(shape, BF if size % 16 == 0 else F32),
        grid_spec=pltpu.PrefetchScalarGridSpec(
            num_scalar_prefetch=1,
            grid=(1,),
            in_specs=[whole(size, width)] * len(pieces),
            out_specs=whole(*shape),
        ),
        compiler_params=PARAMS,
        name="place",
    )(at[None], *pieces).astype(BF)


def first_kernel(at_ref, ends_ref, p1_ref, p2_ref, inner_ref, column_ref, lead_ref, *refs):
    width = inner_ref.shape[0]
    column = (-ends_ref[...]).astype(BF)
    column_ref[...] = column
    lead_ref[...] = jnp.dot(column, inner_ref[...], preferred_element_type=F32)
    refs[-1][:width] = jnp.dot(p1_ref[...], column, preferred_element_type=F32)
    refs[-1][width:] = jnp.dot(p2_ref[...], column, preferred_element_type=F32)
    cut_into(refs[:-1], refs[-1], at_ref[0])


def first_column(at, ends, p1, p2, inner):
    share, width = ends.shape
    return pl.pallas_call(
        first_kernel,
        out_shape=[
            jax.ShapeDtypeStruct((share, width), BF),
            jax.ShapeDtypeStruct((share, width), F32),
            jax.ShapeDtypeStruct((width, width), BF),
            jax.ShapeDtypeStruct((width, width), BF),
        ],
        grid_spec=pltpu.PrefetchScalarGridSpec(
            num_scalar_prefetch=1,
            grid=(1,),
            in_specs=[whole(share, width), whole(width, share), whole(width, share), whole(width, width)],
            out_specs=[whole(share, width)] * 2 + [whole(width, width)] * 2,
            scratch_shapes=[pltpu.VMEM((2 * width, width), F32)],
        ),
        compiler_params=PARAMS,
        name="first_column",
    )(at[None], ends, p1, p2, inner)


def second_kernel(at_ref, ends_ref, lead_ref, p2_ref, column_ref, *refs):
    column = (-(ends_ref[...] + lead_ref[...])).astype(BF)
    column_ref[...] = column
    refs[-1][...] = jnp.dot(p2_ref[...], column, preferred_element_type=F32)
    cut_into(refs[:-1], refs[-1], at_ref[0])


def second_column(at, ends, lead, p2):
    share, width = ends.shape
    return pl.pallas_call(
        second_kernel,
        out_shape=[
            jax.ShapeDtypeStruct((share, width), BF),
            jax.ShapeDtypeStruct((width // 2, width), BF),
            jax.ShapeDtypeStruct((width // 2, width), BF),
        ],
        grid_spec=pltpu.PrefetchScalarGridSpec(
            num_scalar_prefetch=1,
            grid=(1,),
            in_specs=[whole(share, width), whole(share, width), whole(width, share)],
            out_specs=[whole(share, width)] + [whole(width // 2, width)] * 2,
            scratch_shapes=[pltpu.VMEM((width, width), F32)],
        ),
        compiler_params=PARAMS,
        name="second_column",
    )(at[None], ends, lead, p2)


def sharp(left, right):
    high = left.astype(BF)
    rest = left - high.astype(F32)
    middle = rest.astype(BF)
    low = (rest - middle.astype(F32)).astype(BF)
    dot = lambda part: jnp.dot(part, right, preferred_element_type=F32)
    return dot(low) + dot(middle) + dot(high)


def close_kernel(at_ref, low_ref, high_ref, first_ref, second_ref, inner_ref, *refs):
    diagonal_ref, cross_ref, base_ref, sums_ref = refs
    place_into(sums_ref, (low_ref, high_ref), at_ref[0])
    width = inner_ref.shape[0]
    diagonal = first_ref[...] - sums_ref[:width]
    diagonal_ref[...] = diagonal
    cross = -(sharp(diagonal, inner_ref[...]) + sums_ref[width:].T)
    cross_ref[...] = cross
    base_ref[...] = second_ref[...] - sharp(cross.T, inner_ref[...]).T


def close(at, pieces, pivot_first, pivot_second, inner_panel):
    width = inner_panel.shape[0]
    square = whole(width, width)
    return pl.pallas_call(
        close_kernel,
        out_shape=[jax.ShapeDtypeStruct((width, width), F32)] * 3,
        grid_spec=pltpu.PrefetchScalarGridSpec(
            num_scalar_prefetch=1,
            grid=(1,),
            in_specs=[square] * 5,
            out_specs=[square] * 3,
            scratch_shapes=[pltpu.VMEM((2 * width, width), F32)],
        ),
        compiler_params=PARAMS,
        name="close",
    )(at[None], *pieces, pivot_first, pivot_second, inner_panel)


def last_kernel(at_ref, low_ref, high_ref, base_ref, out_ref):
    place_into(out_ref, (low_ref, high_ref), at_ref[0])
    out_ref[...] = base_ref[...] - out_ref[...]


def last(at, pieces, base):
    width = base.shape[0]
    part = whole(width // 2, width)
    return pl.pallas_call(
        last_kernel,
        out_shape=jax.ShapeDtypeStruct((width, width), F32),
        grid_spec=pltpu.PrefetchScalarGridSpec(
            num_scalar_prefetch=1,
            grid=(1,),
            in_specs=[part, part, whole(width, width)],
            out_specs=whole(width, width),
        ),
        compiler_params=PARAMS,
        name="last",
    )(at[None], *pieces, base)


def plan(chips):
    make = lambda rings, start, stop: ("make", rings, start, min(stop, chips))
    step = lambda kind, ring, at: (kind, (ring,), at, at + 1)
    events = [make((0,), 0, 1), step("add", 0, 0), make((0,), 1, 4), step("add", 0, 1)]
    events += [make((1,), 0, 4), step("add", 0, 2), step("add", 1, 0)]
    made = 4
    for at in range(3, chips):
        if made <= at + 1 and made < chips:
            stop = made + 2 if made + 2 >= chips else made + 1
            events.append(make((0, 1), made, stop))
            made = stop
        events += [step("add", 1, at - 2), step("add", 0, at)]
    events += [step("sum", 0, 0), step("add", 1, chips - 2), step("sum", 0, 1)]
    events += [step("add", 1, chips - 1), step("sum", 1, 0), step("sum", 0, 2)]
    for at in range(1, 6):
        events.append(step("sum", 1, at))
        if at < 4:
            events.append(step("sum", 0, at + 2))
    return events


def body(
    ancestor_inverse,
    tile_pattern,
    rows_first,
    rows_second,
    panel_first,
    panel_second,
    inner_panel,
    pivot_first,
    pivot_second,
):
    rows, cols = lax.axis_size("prow"), lax.axis_size("pcol")
    row_id, col_id = lax.axis_index("prow"), lax.axis_index("pcol")
    row_block, col_block = ancestor_inverse.shape
    share = row_block // cols
    half = share // 2
    width = inner_panel.shape[0]
    local = panel_first.shape[1]
    piece = local // rows
    chips = cols // 2

    tile_rows, tile_cols = row_block // TILE, col_block // TILE
    pattern = lax.dynamic_slice(
        tile_pattern, (row_id * tile_rows, col_id * tile_cols), (tile_rows, tile_cols)
    ).reshape(-1)
    chip, core = col_id // 2, col_id % 2
    place = jnp.where(chip % 2 == 0, chip // 2, chips - 1 - chip // 2)
    steps = jnp.arange(chips, dtype=jnp.int32)
    dest = jnp.stack([(place - 1 - steps) % chips, (place + 1 + steps) % chips], axis=1)
    dest = jnp.where(dest < chips // 2, 2 * dest, 2 * (chips - 1 - dest) + 1)
    side = jnp.arange(2, dtype=jnp.int32)[None, :]
    meta = jnp.concatenate(
        [(dest * 2 + core) * 2 + side, (dest * 2 + 1 - core) * 2 + side], axis=1
    ).reshape(-1)
    order = [2 * i if i < chips // 2 else 2 * (chips - 1 - i) + 1 for i in range(chips)]
    onward = [
        (order[i] * 2 + k, order[(i + 1) % chips] * 2 + k) for i in range(chips) for k in range(2)
    ]
    backward = [(b, a) for a, b in onward]
    swap = [(c, c ^ 1) for c in range(cols)]
    to_share = [
        (a * cols + k, k * rows + (a + 1) % rows) for a in range(rows) for k in range(cols)
    ]

    struct_first = lax.dynamic_slice_in_dim(rows_first, row_id * row_block, row_block).astype(BF)
    struct_second = struct_first * lax.dynamic_slice_in_dim(
        rows_second, row_id * row_block, row_block
    ).astype(BF)

    def spread(panel, struct):
        turned = (panel.T * struct[None, :]).reshape(rows, piece, row_block)
        gathered = jnp.zeros((rows, cols // rows, piece, col_block), BF)
        for shift in range(rows):
            part = lax.dynamic_index_in_dim(turned, (row_id + shift) % rows, 0, keepdims=False)
            if shift:
                part = lax.ppermute(part, "prow", [(a, (a + shift) % rows) for a in range(rows)])
            part = part.reshape(piece, cols // rows, col_block).transpose(1, 0, 2)
            gathered = lax.dynamic_update_index_in_dim(gathered, part, (row_id - shift) % rows, 0)
        return gathered.reshape(cols, piece, col_block)

    def exchange(gathered):
        return lax.all_to_all(gathered, "pcol", 0, 0, tiled=True)

    def complete(mine):
        full = jnp.zeros((cols, rows, piece, col_block), BF)
        for shift in range(rows):
            part = mine
            if shift:
                part = lax.ppermute(part, "prow", [(a, (a - shift) % rows) for a in range(rows)])
            full = lax.dynamic_update_index_in_dim(full, part, (row_id + shift) % rows, 1)
        return full.reshape(width, col_block)

    gathered = [spread(panel_first, struct_first), spread(panel_second, struct_second)]
    mine_first = exchange(gathered[0])
    mine_second = exchange(gathered[1])
    panels = [complete(mine_first)]
    panels.append(complete(mine_second))

    own_rows = []
    for number, panel in enumerate(panels):
        own_rows.append(
            lax.ppermute(
                lax.dynamic_slice_in_dim(panel, (row_id + 1) % rows * share, share, 1),
                BOTH,
                to_share,
            )
        )

    made, arrived, ends, summed = [[], []], [[], []], [None, None], [None, None]
    places = (col_id % 2, row_id * 2 + (col_id // 2) % 2, col_id // 4)
    stages = list(zip(stages_of(rows, cols), places))
    for event in plan(chips):
        kind, rings, start, stop = event
        if kind == "make":
            made_now = products(
                start,
                stop,
                meta,
                pattern,
                ancestor_inverse,
                [panels[r] for r in rings],
                half,
                (mine_second,) if rings == (0,) and start == 1 else (),
            )
            theirs = [lax.ppermute(p, "pcol", swap) for p in made_now[len(rings) :]]
            for column, ring in enumerate(rings):
                made[ring] += [(i, made_now[column], theirs[column]) for i in range(stop - start)]
        elif kind == "add":
            ring = rings[0]
            total = add(*made[ring][start], arrived[ring], start == chips - 1)
            if start == chips - 1:
                ends[ring] = total[0].reshape(share, width)
            else:
                arrived[ring] = [
                    lax.ppermute(total[0], "pcol", onward),
                    lax.ppermute(total[1], "pcol", backward),
                ]
        else:
            ring, number = rings[0], start
            (members, group), at = stages[min(number, 5 - number)]
            if number == 0 and ring == 0:
                column_first, lead, *cuts = first_column(at, ends[0], *own_rows, inner_panel)
            elif number == 0:
                column_second, *cuts = second_column(at, ends[1], lead, own_rows[1])
            elif number == 1:
                cuts = cut(at, members, summed[ring])
            elif number < 4:
                cuts = cut(at, 1, summed[ring])
            elif number == 4:
                cuts = [place_all(stages[1][1], summed[ring])]
            elif ring == 0:
                diagonal_first, inner_second, base = close(
                    at, summed[0], pivot_first, pivot_second, inner_panel
                )
            else:
                diagonal_second = last(at, summed[1], base)
            if number < 5:
                (members, group), _ = stages[(0, 1, 2, 1, 0)[number]]
                summed[ring] = [cuts[0]] + [
                    to_follower(
                        cuts[shift] if number < 2 else cuts[0],
                        rows,
                        cols,
                        members,
                        group,
                        shift if number < 2 else members - shift,
                    )
                    for shift in range(1, members)
                ]
    return (column_first, diagonal_first, inner_second, column_second, diagonal_second)


def solution(mesh):
    return jax.shard_map(
        body,
        mesh=mesh,
        in_specs=(
            P("prow", "pcol"),
            P(),
            P(),
            P(),
            P("prow", "pcol"),
            P("prow", "pcol"),
            P(),
            P(),
            P(),
        ),
        out_specs=(P(("prow", "pcol"), None), P(), P(), P(("prow", "pcol"), None), P()),
        check_vma=False,
    )
```
